32 devices in a mesh: grp: 2 (over x), blk: 16 (over z, y, core).
Axes of the slice: x: 2, y: 2, z: 4, core: 2. Of those that a mesh axis runs over, the one named last changes fastest.
Arguments:
- sketch: bfloat16 [256, 131072], P(None, 'blk'), may hold values from -3 to 3
- leaf_maps: bfloat16 [2, 16, 256, 256], P('grp', 'blk')
- mix_maps: bfloat16 [2, 64, 16, 16], P('grp', 'blk')
Outputs:
- sketch_update: bfloat16 [256, 131072], P('grp', 'blk')
The draws below stay inside these ranges and needn't reach their ends.
All inputs are finite; a program needn't handle non-finite values.
Results may differ from the reference program's by a relative error of at most 0.015.
Values may be sent and summed in bfloat16 or wider, within the bound.
A program may use at most 64 MiB of HBM per device.

```python
import math
import jax
import jax.numpy as jnp
from jax import lax

B = 128
R = 256
A = 64
N = 131072
N_GRP = 2
N_BLK = 16


def draw_leaf_maps(key, part):
    leaf_side = 2 * B
    full_shape = (N_GRP, N_BLK, leaf_side, leaf_side)
    random_part = jax.random.normal(key, full_shape, jnp.float32)
    identity = jnp.eye(leaf_side, dtype=jnp.float32)
    return (identity + 0.3 / math.sqrt(leaf_side) * random_part).astype(jnp.bfloat16)


def draw_mix_maps(key, part):
    full_shape = (N_GRP, A, N_BLK, N_BLK)
    random_part = jax.random.normal(key, full_shape, jnp.float32)
    identity = jnp.eye(N_BLK, dtype=jnp.float32)
    return (identity + 0.3 / math.sqrt(N_BLK) * random_part).astype(jnp.bfloat16)


def level_of(key, extent, split, low, top_value):
    def one(dim, parts):
        draws = jax.random.uniform(jax.random.fold_in(jax.random.fold_in(key, 6), dim), (parts,), jnp.float32, low / len(split), top_value / len(split))
        return jnp.repeat(jnp.exp(draws), extent[dim] // parts).reshape((-1,) + (1,) * (len(extent) - dim - 1))

    factor_of = one(*split[0])
    for cut in split[1:]:
        factor_of = factor_of * one(*cut)
    return factor_of


def bell_draw(stream_key, extent, deviation, most, shards=(), kind=jnp.bfloat16):
    values = jax.random.normal(stream_key, extent, jnp.float32) * deviation
    if len(shards) > 0:
        values = level_of(stream_key, extent, shards, -0.22, 0.18) * values
    return jnp.clip(values, min=-most, max=most).astype(kind)


def setup_inputs(seed: int = 0) -> dict:
    seeds = jax.random.split(jax.random.key(seed), 4)
    sketch = bell_draw(seeds[0], (R, N), 0.5, 3.0, ((1, 16),))
    leaf_maps = draw_leaf_maps(jax.random.fold_in(seeds[3], 71), 0)
    mix_maps = draw_mix_maps(jax.random.fold_in(seeds[3], 71), 0)
    return dict(sketch=sketch, leaf_maps=leaf_maps, mix_maps=mix_maps)


def apply_section(current, leaf_map, mixing):
    columns, blocks, leaves, sub_rows = current.shape
    low_part = leaves // blocks
    paired = current.reshape(columns, blocks, leaves // 2, 2 * sub_rows).astype(jnp.float32)
    product = jnp.einsum("rdmi,dij->rdmj", paired, leaf_map.astype(jnp.float32)).astype(jnp.bfloat16)
    product = product.reshape(columns, blocks, blocks, low_part, sub_rows).astype(jnp.float32)
    weights = mixing.reshape(blocks, low_part, blocks, blocks).astype(jnp.float32)
    result = jnp.einsum("dlhk,rdklb->rdhlb", weights, product).astype(jnp.bfloat16)
    return jnp.transpose(result, (0, 2, 1, 3, 4)).reshape(columns, blocks, leaves, sub_rows)


def reference(sketch, leaf_maps, mix_maps):
    panel_cols = sketch.reshape(R // 16, 16, N_BLK, A, B)

    def run_chain(current):
        for section_index in range(N_GRP):
            current = apply_section(current, leaf_maps[section_index], mix_maps[section_index])
        return current

    return lax.map(run_chain, panel_cols).reshape(R, N)
```

```python
import functools

import jax
import jax.numpy as jnp
from jax import lax
from jax.experimental import pallas as pl
from jax.experimental.pallas import tpu as pltpu
from jax.sharding import PartitionSpec as P

MESH = pl.DeviceIdType.MESH
TILE = 16


def chain_kernel(
    groups, blocks, sketch_ref, leaf_in, mix_in, out_ref,
    x_vm, send, recv, half, leaf_all, mix_all, weights,
    x_sem, send_sem, recv_sem, leaf_send, leaf_recv, mix_send, mix_recv,
):
    grp = lax.axis_index("grp")
    blk = lax.axis_index("blk")
    chunks, rows, row_len = x_vm.shape
    sub = leaf_in.shape[0] // 2
    leaves = row_len // sub
    low = leaves // blocks
    wide = low * sub
    tiles = rows // TILE

    barrier = pltpu.get_barrier_semaphore()
    for step in range(1, blocks):
        pl.semaphore_signal(
            barrier, inc=1, device_id={"blk": lax.rem(blk + step, blocks)}, device_id_type=MESH
        )
    for step in range(1, groups):
        pl.semaphore_signal(
            barrier, inc=1, device_id={"grp": lax.rem(grp + step, groups)}, device_id_type=MESH
        )

    def load(chunk):
        start = pl.multiple_of(grp * (chunks * rows) + chunk * rows, TILE)
        return pltpu.make_async_copy(
            sketch_ref.at[pl.ds(start, rows), :], x_vm.at[chunk], x_sem.at[chunk]
        )

    for chunk in range(chunks):
        load(chunk).start()

    pl.semaphore_wait(barrier, blocks - 1 + groups - 1)

    def factor_copies(step):
        partner = lax.rem(grp + step, groups)
        return (
            pltpu.make_async_remote_copy(
                leaf_in, leaf_all.at[grp], leaf_send.at[step], leaf_recv.at[step],
                device_id={"grp": partner}, device_id_type=MESH),
            pltpu.make_async_remote_copy(
                mix_in, mix_all.at[grp], mix_send.at[step], mix_recv.at[step],
                device_id={"grp": partner}, device_id_type=MESH),
        )

    for step in range(1, groups):
        for copy in factor_copies(step):
            copy.start()
    leaf_all[grp] = leaf_in[...]
    mix_all[grp] = mix_in[...]
    for step in range(1, groups):
        for copy in factor_copies(step):
            copy.wait()

    big = blocks * TILE
    spread = (
        lax.broadcasted_iota(jnp.int32, (big, blocks), 0) // TILE
        == lax.broadcasted_iota(jnp.int32, (big, blocks), 1)
    ).astype(jnp.bfloat16)
    same = (
        lax.broadcasted_iota(jnp.int32, (big, big), 0) % TILE
        == lax.broadcasted_iota(jnp.int32, (big, big), 1) % TILE
    )

    def build_weights(section):
        for l in range(low):
            mix = mix_all[section, pl.ds(l * blocks, blocks), :]
            tall = jnp.dot(spread, mix, preferred_element_type=jnp.float32).astype(jnp.bfloat16)
            full = lax.dot_general(
                tall, spread, (((1,), (1,)), ((), ())), preferred_element_type=jnp.float32)
            weights[l] = jnp.where(same, full, 0.0).astype(jnp.bfloat16)

    order = sorted(range(1, blocks), key=lambda step: (abs(step - blocks // 2), step))

    for section in range(groups):
        last = section == groups - 1
        build_weights(section)

        @pl.loop(0, chunks)
        def _(chunk):
            if section == 0:
                load(chunk).wait()
            else:
                arrived = recv.at[section - 1, chunk]
                pltpu.make_async_copy(arrived, arrived, recv_sem.at[section - 1, chunk]).wait()

            def piece(leaf):
                if section == 0:
                    return x_vm[chunk, :, pl.ds(leaf * sub, sub)]
                return recv[section - 1, chunk, leaf // low, :, pl.ds(leaf % low * sub, sub)]

            leaf_map = leaf_all[section]
            per = min(leaves // 2, max(1, 256 // rows))
            for first in range(0, leaves // 2, per):
                lhs = jnp.concatenate(
                    [jnp.concatenate([piece(2 * m), piece(2 * m + 1)], axis=1)
                     for m in range(first, first + per)], axis=0)
                product = jnp.dot(
                    lhs, leaf_map, preferred_element_type=jnp.float32).astype(jnp.bfloat16)
                for i in range(per):
                    for j in range(2):
                        half[2 * (first + i) + j] = product[
                            i * rows:(i + 1) * rows, j * sub:(j + 1) * sub]

            for l in range(low):
                rhs = jnp.concatenate(
                    [jnp.concatenate(
                        [half[k * low + l, pl.ds(t * TILE, TILE), :] for t in range(tiles)], axis=1)
                     for k in range(blocks)], axis=0)
                mixed = jnp.dot(
                    weights[l], rhs, preferred_element_type=jnp.float32).astype(jnp.bfloat16)
                for h in range(blocks):
                    for t in range(tiles):
                        send[section, chunk, h, pl.ds(t * TILE, TILE), pl.ds(l * sub, sub)] = mixed[
                            h * TILE:(h + 1) * TILE, t * sub:(t + 1) * sub]

            if last:
                place = out_ref.at[
                    pl.ds(pl.multiple_of(chunk * rows, TILE), rows),
                    pl.ds(pl.multiple_of(blk * wide, sub), wide)]
            else:
                place = recv.at[section, chunk, blk]
            for step in order:
                target = lax.rem(blk + step, blocks)
                pltpu.make_async_remote_copy(
                    send.at[section, chunk, target], place,
                    send_sem.at[section, chunk], recv_sem.at[section, chunk],
                    device_id={"blk": target}, device_id_type=MESH).start()
            pltpu.make_async_copy(
                send.at[section, chunk, blk], place, recv_sem.at[section, chunk]).start()

    @pl.loop(0, chunks)
    def _(chunk):
        arrived = out_ref.at[pl.ds(pl.multiple_of(chunk * rows, TILE), rows), :]
        pltpu.make_async_copy(arrived, arrived, recv_sem.at[groups - 1, chunk]).wait()
        for section in range(groups):
            left = send.at[section, chunk, pl.ds(0, blocks - 1)]
            pltpu.make_async_copy(left, left, send_sem.at[section, chunk]).wait()


def on_device(sketch, leaf_maps, mix_maps):
    groups, blocks = lax.axis_size("grp"), lax.axis_size("blk")
    total_cols, rows_dev = sketch.shape
    own_cols = total_cols // groups
    pair = leaf_maps.shape[2]
    sub = pair // 2
    leaves = rows_dev // sub
    low = leaves // blocks
    rows = min(2 * TILE, own_cols)
    chunks = own_cols // rows
    big = blocks * TILE
    any_space = pl.BlockSpec(memory_space=pl.ANY)
    in_vmem = pl.BlockSpec(memory_space=pltpu.VMEM)
    dma = pltpu.SemaphoreType.DMA
    bf16 = jnp.bfloat16
    return pl.pallas_call(
        functools.partial(chain_kernel, groups, blocks),
        out_shape=jax.ShapeDtypeStruct((own_cols, rows_dev), bf16),
        in_specs=[any_space, in_vmem, in_vmem],
        out_specs=any_space,
        scratch_shapes=[
            pltpu.VMEM((chunks, rows, rows_dev), bf16),
            pltpu.VMEM((groups, chunks, blocks, rows, low * sub), bf16),
            pltpu.VMEM((groups - 1, chunks, blocks, rows, low * sub), bf16),
            pltpu.VMEM((leaves, rows, sub), bf16),
            pltpu.VMEM((groups, pair, pair), bf16),
            pltpu.VMEM((groups, low * blocks, blocks), bf16),
            pltpu.VMEM((low, big, big), bf16),
            dma((chunks,)),
            dma((groups, chunks)),
            dma((groups, chunks)),
            dma((groups,)), dma((groups,)), dma((groups,)), dma((groups,)),
        ],
        compiler_params=pltpu.CompilerParams(
            collective_id=0, has_side_effects=True, vmem_limit_bytes=48 * 1024 * 1024),
    )(sketch, leaf_maps.reshape(pair, pair), mix_maps.reshape(low * blocks, blocks))


def solution(mesh):
    placed = (P(None, "blk"), P("grp", "blk", None, None), P("grp", "blk", None, None))
    return jax.shard_map(
        on_device, mesh=mesh, in_specs=placed, out_specs=P("grp", "blk"), check_vma=False
    )
```

```python
import functools

import jax
import jax.numpy as jnp
from jax import lax
from jax.experimental import pallas as pl
from jax.experimental.pallas import tpu as pltpu
from jax.sharding import PartitionSpec as P

MESH = pl.DeviceIdType.MESH
TILE = 16
LANES = 128


def chunk_rows(own_cols):
    left, sizes = own_cols, []
    for size in CHUNKS:
        if left >= size:
            sizes.append(size)
            left -= size
    while left > 0:
        sizes.append(min(left, 2 * TILE))
        left -= sizes[-1]
    return sizes


CHUNKS = (16,16,32,64)


def chain_kernel(
    groups, blocks, sizes, sketch_ref, leaf_in, mix_in, out_ref,
    x_vm, send, recv, half, leaf_all, mix_vm, mix_all, weights,
    x_sem, send_sem, recv_sem, own_sem, leaf_send, leaf_recv, mix_send, mix_recv, go_sem,
):
    grp = lax.axis_index("grp")
    blk = lax.axis_index("blk")
    own_cols, row_len = x_vm.shape
    sub = leaf_in.shape[0] // 2
    leaves = row_len // sub
    low = leaves // blocks
    wide = low * sub
    starts = [sum(sizes[:i]) for i in range(len(sizes))]
    big = blocks * TILE

    barrier = pltpu.get_barrier_semaphore()

    def greet(**where):
        pl.semaphore_signal(barrier, inc=1, device_id=where, device_id_type=MESH)

    @pl.when(grp == 0)
    def _():
        for step in range(blocks):
            greet(grp=1, blk=lax.rem(blk + step, blocks))
        for other in range(2, groups):
            greet(grp=other, blk=blk)

    @pl.when(grp > 0)
    def _():
        for step in range(1, groups):
            greet(grp=lax.rem(grp + step, groups), blk=blk)
        for step in range(1, blocks):
            greet(grp=grp, blk=lax.rem(blk + step, blocks))

    own_mix = pltpu.make_async_copy(mix_in, mix_vm, own_sem.at[0])
    own_leaf = pltpu.make_async_copy(leaf_in, leaf_all.at[grp], own_sem.at[1])
    own_mix.start()
    own_leaf.start()

    def load(chunk):
        rows = pl.ds(pl.multiple_of(grp * own_cols + starts[chunk], TILE), sizes[chunk])
        return pltpu.make_async_copy(
            sketch_ref.at[rows, :], x_vm.at[pl.ds(starts[chunk], sizes[chunk]), :], x_sem.at[chunk])

    for chunk in range(len(sizes)):
        load(chunk).start()

    own_mix.wait()
    pick = (
        lax.broadcasted_iota(jnp.int32, (blocks, blocks), 0)
        == lax.broadcasted_iota(jnp.int32, (blocks, blocks), 1)
    ).astype(jnp.bfloat16)
    mix_all[grp] = jnp.zeros(mix_all.shape[1:], jnp.bfloat16)
    mix_all[grp, :, pl.ds(0, low * blocks)] = lax.dot_general(
        pick, mix_vm[...], (((1,), (1,)), ((), ())), preferred_element_type=jnp.float32
    ).astype(jnp.bfloat16)
    own_leaf.wait()

    def factor_copies(target, owner):
        where = {"grp": target}
        return (
            pltpu.make_async_remote_copy(
                leaf_in, leaf_all.at[owner], leaf_send.at[target], leaf_recv.at[owner],
                device_id=where, device_id_type=MESH),
            pltpu.make_async_remote_copy(
                mix_all.at[owner], mix_all.at[owner], mix_send.at[target], mix_recv.at[owner],
                device_id=where, device_id_type=MESH),
        )

    def send_factors():
        for step in range(1, groups):
            for copy in factor_copies(lax.rem(grp + step, groups), grp):
                copy.start()

    @pl.when(grp == 0)
    def _():
        pl.semaphore_wait(barrier, groups - 1)
        send_factors()

    @pl.when(grp == 1)
    def _():
        pl.semaphore_wait(barrier, 2 * blocks - 1 + groups - 2)
        pl.semaphore_signal(go_sem, inc=1, device_id={"grp": 0}, device_id_type=MESH)
        send_factors()

    @pl.when(grp > 1)
    def _():
        pl.semaphore_wait(barrier, blocks - 1 + groups - 1)
        send_factors()

    spread = (
        lax.broadcasted_iota(jnp.int32, (big, blocks), 0) // TILE
        == lax.broadcasted_iota(jnp.int32, (big, blocks), 1)
    ).astype(jnp.bfloat16)
    same = (
        lax.broadcasted_iota(jnp.int32, (big, big), 0) % TILE
        == lax.broadcasted_iota(jnp.int32, (big, big), 1) % TILE
    )
    nums = (((1,), (1,)), ((), ()))
    width = mix_all.shape[2]

    def build_weights(section):
        for l in range(low):
            chosen = (
                lax.broadcasted_iota(jnp.int32, (big, width), 0) // TILE + l * blocks
                == lax.broadcasted_iota(jnp.int32, (big, width), 1)
            ).astype(jnp.bfloat16)
            tall = lax.dot_general(
                chosen, mix_all[section], nums, preferred_element_type=jnp.float32
            ).astype(jnp.bfloat16)
            full = lax.dot_general(tall, spread, nums, preferred_element_type=jnp.float32)
            weights[l] = jnp.where(same, full, 0.0).astype(jnp.bfloat16)

    def compute(section, start, rows):
        unit = pl.ds(start, rows)
        tiles = rows // TILE

        def piece(leaf):
            if section == 0:
                return x_vm[unit, pl.ds(leaf * sub, sub)]
            return recv[section - 1, leaf // low, unit, pl.ds(leaf % low * sub, sub)]

        leaf_map = leaf_all[section]
        per = min(leaves // 2, max(1, 256 // rows))
        for first in range(0, leaves // 2, per):
            lhs = jnp.concatenate(
                [jnp.concatenate([piece(2 * m), piece(2 * m + 1)], axis=1)
                 for m in range(first, first + per)], axis=0)
            product = jnp.dot(
                lhs, leaf_map, preferred_element_type=jnp.float32).astype(jnp.bfloat16)
            for i in range(per):
                for j in range(2):
                    half[2 * (first + i) + j, pl.ds(0, rows), :] = product[
                        i * rows:(i + 1) * rows, j * sub:(j + 1) * sub]

        for l in range(low):
            rhs = jnp.concatenate(
                [jnp.concatenate(
                    [half[k * low + l, pl.ds(t * TILE, TILE), :] for t in range(tiles)], axis=1)
                 for k in range(blocks)], axis=0)
            mixed = jnp.dot(
                weights[l], rhs, preferred_element_type=jnp.float32).astype(jnp.bfloat16)
            for h in range(blocks):
                for t in range(tiles):
                    send[section, h, pl.ds(start + t * TILE, TILE), pl.ds(l * sub, sub)] = mixed[
                        h * TILE:(h + 1) * TILE, t * sub:(t + 1) * sub]

    order = sorted(range(1, blocks), key=lambda step: (abs(step - blocks // 2), step))

    for section in range(groups):
        @pl.when(grp != section)
        def _():
            for copy in factor_copies(section, section):
                copy.wait_recv()

        build_weights(section)

        for chunk, (start, rows) in enumerate(zip(starts, sizes)):
            span = pl.ds(start, rows)
            if section == 0:
                load(chunk).wait()
            else:
                arrived = recv.at[section - 1, :, span, :]
                pltpu.make_async_copy(arrived, arrived, recv_sem.at[section - 1, chunk]).wait()

            unit = half.shape[1]
            if rows <= unit:
                compute(section, start, rows)
            else:
                @pl.loop(0, rows // unit)
                def _(i):
                    compute(section, pl.multiple_of(start + i * unit, TILE), unit)

            if section == 0 and chunk == 0:
                @pl.when(grp == 0)
                def _():
                    pl.semaphore_wait(go_sem, 1)

            if section == groups - 1:
                place = out_ref.at[span, pl.ds(pl.multiple_of(blk * wide, sub), wide)]
            else:
                place = recv.at[section, blk, span, :]
            for step in order:
                target = lax.rem(blk + step, blocks)
                pltpu.make_async_remote_copy(
                    send.at[section, target, span, :], place,
                    send_sem.at[section, chunk], recv_sem.at[section, chunk],
                    device_id={"blk": target}, device_id_type=MESH).start()
            pltpu.make_async_copy(
                send.at[section, blk, span, :], place, recv_sem.at[section, chunk]).start()

    for step in range(1, groups):
        for copy in factor_copies(lax.rem(grp + step, groups), grp):
            copy.wait_send()
    for chunk, (start, rows) in enumerate(zip(starts, sizes)):
        span = pl.ds(start, rows)
        for section in range(groups):
            left = send.at[section, pl.ds(0, blocks - 1), span, :]
            pltpu.make_async_copy(left, left, send_sem.at[section, chunk]).wait()
        arrived = out_ref.at[span, :]
        pltpu.make_async_copy(arrived, arrived, recv_sem.at[groups - 1, chunk]).wait()


def on_device(sketch, leaf_maps, mix_maps):
    groups, blocks = lax.axis_size("grp"), lax.axis_size("blk")
    total_cols, rows_dev = sketch.shape
    own_cols = total_cols // groups
    pair = leaf_maps.shape[2]
    sub = pair // 2
    leaves = rows_dev // sub
    low = leaves // blocks
    sizes = chunk_rows(own_cols)
    big = blocks * TILE
    width = -(-low * blocks // LANES) * LANES
    in_hbm = pl.BlockSpec(memory_space=pltpu.HBM)
    dma = pltpu.SemaphoreType.DMA
    bf16 = jnp.bfloat16
    return pl.pallas_call(
        functools.partial(chain_kernel, groups, blocks, sizes),
        out_shape=jax.ShapeDtypeStruct((own_cols, rows_dev), bf16),
        in_specs=[in_hbm, in_hbm, in_hbm],
        out_specs=pl.BlockSpec(memory_space=pl.ANY),
        scratch_shapes=[
            pltpu.VMEM((own_cols, rows_dev), bf16),
            pltpu.VMEM((groups, blocks, own_cols, low * sub), bf16),
            pltpu.VMEM((groups - 1, blocks, own_cols, low * sub), bf16),
            pltpu.VMEM((leaves, 2 * TILE, sub), bf16),
            pltpu.VMEM((groups, pair, pair), bf16),
            pltpu.VMEM((low * blocks, blocks), bf16),
            pltpu.VMEM((groups, blocks, width), bf16),
            pltpu.VMEM((low, big, big), bf16),
            dma((len(sizes),)),
            dma((groups, len(sizes))),
            dma((groups, len(sizes))),
            dma((2,)),
            dma((groups,)), dma((groups,)), dma((groups,)), dma((groups,)),
            pltpu.SemaphoreType.REGULAR,
        ],
        compiler_params=pltpu.CompilerParams(
            collective_id=0, has_side_effects=True, vmem_limit_bytes=48 * 1024 * 1024),
    )(sketch, leaf_maps.reshape(pair, pair), mix_maps.reshape(low * blocks, blocks))


def solution(mesh):
    placed = (P(None, "blk"), P("grp", "blk", None, None), P("grp", "blk", None, None))
    return jax.shard_map(
        on_device, mesh=mesh, in_specs=placed, out_specs=P("grp", "blk"), check_vma=False
    )
```

```python
import functools

import jax
import jax.numpy as jnp
from jax import lax
from jax.experimental import pallas as pl
from jax.experimental.pallas import tpu as pltpu
from jax.sharding import PartitionSpec as P

MESH = pl.DeviceIdType.MESH
TILE = 16
LANES = 128


def chunk_rows(own_cols):
    left, sizes = own_cols, []
    for size in CHUNKS:
        if left >= size:
            sizes.append(size)
            left -= size
    while left > 0:
        sizes.append(min(left, 2 * TILE))
        left -= sizes[-1]
    return sizes


CHUNKS = (16,16,32,64)


def chain_kernel(
    groups, blocks, sizes, sketch_ref, leaf_in, mix_in, out_ref,
    x_vm, send, recv, half, leaf_all, mix_vm, mix_all, weights,
    x_sem, send_sem, recv_sem, own_sem, leaf_send, leaf_recv, mix_send, mix_recv, go_sem,
):
    grp = lax.axis_index("grp")
    blk = lax.axis_index("blk")
    own_cols, row_len = x_vm.shape
    sub = leaf_in.shape[0] // 2
    leaves = row_len // sub
    low = leaves // blocks
    wide = low * sub
    starts = [sum(sizes[:i]) for i in range(len(sizes))]
    big = blocks * TILE

    barrier = pltpu.get_barrier_semaphore()

    def greet(**where):
        pl.semaphore_signal(barrier, inc=1, device_id=where, device_id_type=MESH)

    @pl.when(grp == 0)
    def _():
        for step in range(blocks):
            greet(grp=1, blk=lax.rem(blk + step, blocks))
        for other in range(2, groups):
            greet(grp=other, blk=blk)

    @pl.when(grp > 0)
    def _():
        for step in range(1, groups):
            greet(grp=lax.rem(grp + step, groups), blk=blk)
        for step in range(1, blocks):
            greet(grp=grp, blk=lax.rem(blk + step, blocks))

    own_mix = pltpu.make_async_copy(mix_in, mix_vm, own_sem.at[0])
    own_leaf = pltpu.make_async_copy(leaf_in, leaf_all.at[grp], own_sem.at[1])
    own_mix.start()
    own_leaf.start()

    def load(chunk):
        rows = pl.ds(pl.multiple_of(grp * own_cols + starts[chunk], TILE), sizes[chunk])
        return pltpu.make_async_copy(
            sketch_ref.at[rows, :], x_vm.at[pl.ds(starts[chunk], sizes[chunk]), :], x_sem.at[chunk])

    for chunk in range(len(sizes)):
        load(chunk).start()

    own_mix.wait()
    pick = (
        lax.broadcasted_iota(jnp.int32, (blocks, blocks), 0)
        == lax.broadcasted_iota(jnp.int32, (blocks, blocks), 1)
    ).astype(jnp.bfloat16)
    mix_all[grp] = jnp.zeros(mix_all.shape[1:], jnp.bfloat16)
    mix_all[grp, :, pl.ds(0, low * blocks)] = lax.dot_general(
        pick, mix_vm[...], (((1,), (1,)), ((), ())), preferred_element_type=jnp.float32
    ).astype(jnp.bfloat16)
    def factor_copies(target, owner):
        where = {"grp": target}
        return (
            pltpu.make_async_remote_copy(
                mix_all.at[owner], mix_all.at[owner], mix_send.at[target], mix_recv.at[owner],
                device_id=where, device_id_type=MESH),
            pltpu.make_async_remote_copy(
                leaf_in, leaf_all.at[owner], leaf_send.at[target], leaf_recv.at[owner],
                device_id=where, device_id_type=MESH),
        )

    def send_factors():
        for step in range(1, groups):
            for copy in factor_copies(lax.rem(grp + step, groups), grp):
                copy.start()

    @pl.when(grp == 0)
    def _():
        pl.semaphore_wait(barrier, groups - 1)
        send_factors()

    @pl.when(grp == 1)
    def _():
        pl.semaphore_wait(barrier, 2 * blocks - 1 + groups - 2)
        pl.semaphore_signal(go_sem, inc=1, device_id={"grp": 0}, device_id_type=MESH)

    @pl.when(grp > 1)
    def _():
        pl.semaphore_wait(barrier, blocks - 1 + groups - 1)

    spread = (
        lax.broadcasted_iota(jnp.int32, (big, blocks), 0) // TILE
        == lax.broadcasted_iota(jnp.int32, (big, blocks), 1)
    ).astype(jnp.bfloat16)
    same = (
        lax.broadcasted_iota(jnp.int32, (big, big), 0) % TILE
        == lax.broadcasted_iota(jnp.int32, (big, big), 1) % TILE
    )
    nums = (((1,), (1,)), ((), ()))
    width = mix_all.shape[2]

    def build_weights(section):
        for l in range(low):
            chosen = (
                lax.broadcasted_iota(jnp.int32, (big, width), 0) // TILE + l * blocks
                == lax.broadcasted_iota(jnp.int32, (big, width), 1)
            ).astype(jnp.bfloat16)
            tall = lax.dot_general(
                chosen, mix_all[section], nums, preferred_element_type=jnp.float32
            ).astype(jnp.bfloat16)
            full = lax.dot_general(tall, spread, nums, preferred_element_type=jnp.float32)
            weights[l] = jnp.where(same, full, 0.0).astype(jnp.bfloat16)

    def compute(section, start, rows):
        unit = pl.ds(start, rows)
        tiles = rows // TILE

        def piece(leaf):
            if section == 0:
                return x_vm[unit, pl.ds(leaf * sub, sub)]
            return recv[section - 1, leaf // low, unit, pl.ds(leaf % low * sub, sub)]

        leaf_map = leaf_all[section]
        per = min(leaves // 2, max(1, 256 // rows))
        for first in range(0, leaves // 2, per):
            lhs = jnp.concatenate(
                [jnp.concatenate([piece(2 * m), piece(2 * m + 1)], axis=1)
                 for m in range(first, first + per)], axis=0)
            product = jnp.dot(
                lhs, leaf_map, preferred_element_type=jnp.float32).astype(jnp.bfloat16)
            for i in range(per):
                for j in range(2):
                    half[2 * (first + i) + j, pl.ds(0, rows), :] = product[
                        i * rows:(i + 1) * rows, j * sub:(j + 1) * sub]

        for l in range(low):
            rhs = jnp.concatenate(
                [jnp.concatenate(
                    [half[k * low + l, pl.ds(t * TILE, TILE), :] for t in range(tiles)], axis=1)
                 for k in range(blocks)], axis=0)
            mixed = jnp.dot(
                weights[l], rhs, preferred_element_type=jnp.float32).astype(jnp.bfloat16)
            for h in range(blocks):
                for t in range(tiles):
                    send[section, h, pl.ds(start + t * TILE, TILE), pl.ds(l * sub, sub)] = mixed[
                        h * TILE:(h + 1) * TILE, t * sub:(t + 1) * sub]

    order = list(range(1, blocks))

    for section in range(groups):
        @pl.when(grp != section)
        def _():
            factor_copies(section, section)[0].wait_recv()

        build_weights(section)

        @pl.when(grp != section)
        def _():
            factor_copies(section, section)[1].wait_recv()

        @pl.when(grp == section)
        def _():
            own_leaf.wait()

        for chunk, (start, rows) in enumerate(zip(starts, sizes)):
            span = pl.ds(start, rows)
            if section == 0:
                load(chunk).wait()
            else:
                arrived = recv.at[section - 1, :, span, :]
                pltpu.make_async_copy(arrived, arrived, recv_sem.at[section - 1, chunk]).wait()

            unit = half.shape[1]
            if rows <= unit:
                compute(section, start, rows)
            else:
                @pl.loop(0, rows // unit)
                def _(i):
                    compute(section, pl.multiple_of(start + i * unit, TILE), unit)

            if section == 0 and chunk == 0:
                @pl.when(grp == 0)
                def _():
                    pl.semaphore_wait(go_sem, 1)

                @pl.when(grp > 0)
                def _():
                    send_factors()

            if section == groups - 1:
                place = out_ref.at[span, pl.ds(pl.multiple_of(blk * wide, sub), wide)]
            else:
                place = recv.at[section, blk, span, :]
            for step in order:
                target = lax.rem(blk + step, blocks)
                pltpu.make_async_remote_copy(
                    send.at[section, target, span, :], place,
                    send_sem.at[section, chunk], recv_sem.at[section, chunk],
                    device_id={"blk": target}, device_id_type=MESH).start()
            pltpu.make_async_copy(
                send.at[section, blk, span, :], place, recv_sem.at[section, chunk]).start()

    for step in range(1, groups):
        for copy in factor_copies(lax.rem(grp + step, groups), grp):
            copy.wait_send()
    for chunk, (start, rows) in enumerate(zip(starts, sizes)):
        span = pl.ds(start, rows)
        for section in range(groups):
            left = send.at[section, pl.ds(0, blocks - 1), span, :]
            pltpu.make_async_copy(left, left, send_sem.at[section, chunk]).wait()
        arrived = out_ref.at[span, :]
        pltpu.make_async_copy(arrived, arrived, recv_sem.at[groups - 1, chunk]).wait()


def on_device(sketch, leaf_maps, mix_maps):
    groups, blocks = lax.axis_size("grp"), lax.axis_size("blk")
    total_cols, rows_dev = sketch.shape
    own_cols = total_cols // groups
    pair = leaf_maps.shape[2]
    sub = pair // 2
    leaves = rows_dev // sub
    low = leaves // blocks
    sizes = chunk_rows(own_cols)
    big = blocks * TILE
    width = -(-low * blocks // LANES) * LANES
    in_hbm = pl.BlockSpec(memory_space=pltpu.HBM)
    dma = pltpu.SemaphoreType.DMA
    bf16 = jnp.bfloat16
    return pl.pallas_call(
        functools.partial(chain_kernel, groups, blocks, sizes),
        out_shape=jax.ShapeDtypeStruct((own_cols, rows_dev), bf16),
        in_specs=[in_hbm, in_hbm, in_hbm],
        out_specs=pl.BlockSpec(memory_space=pl.ANY),
        scratch_shapes=[
            pltpu.VMEM((own_cols, rows_dev), bf16),
            pltpu.VMEM((groups, blocks, own_cols, low * sub), bf16),
            pltpu.VMEM((groups - 1, blocks, own_cols, low * sub), bf16),
            pltpu.VMEM((leaves, 2 * TILE, sub), bf16),
            pltpu.VMEM((groups, pair, pair), bf16),
            pltpu.VMEM((low * blocks, blocks), bf16),
            pltpu.VMEM((groups, blocks, width), bf16),
            pltpu.VMEM((low, big, big), bf16),
            dma((len(sizes),)),
            dma((groups, len(sizes))),
            dma((groups, len(sizes))),
            dma((2,)),
            dma((groups,)), dma((groups,)), dma((groups,)), dma((groups,)),
            pltpu.SemaphoreType.REGULAR,
        ],
        compiler_params=pltpu.CompilerParams(
            collective_id=0, has_side_effects=True, vmem_limit_bytes=48 * 1024 * 1024),
    )(sketch, leaf_maps.reshape(pair, pair), mix_maps.reshape(low * blocks, blocks))


def solution(mesh):
    placed = (P(None, "blk"), P("grp", "blk", None, None), P("grp", "blk", None, None))
    return jax.shard_map(
        on_device, mesh=mesh, in_specs=placed, out_specs=P("grp", "blk"), check_vma=False
    )
```
